32 devices in a mesh: seq: 16 (over z, x, core), head: 2 (over y).
Axes of the slice: x: 2, y: 2, z: 4, core: 2. Of those that a mesh axis runs over, the one named last changes fastest.
Arguments:
- alignment_rows: bfloat16 [128, 1024, 256], P('seq'), may hold values from -16 to 16
- upstream_derivative_tensor: bfloat16 [128, 1024, 256], P(None, 'seq'), may hold values from -12 to 12
- saved_pair_bias: bfloat16 [8, 1024, 1024], P('head', 'seq'), may hold values from -360 to 360
- pairwise_features: bfloat16 [1024, 1024, 128], P('seq', 'head'), may hold values from -16 to 16
- sequence_layernorm_scaling: float32 [256], replicated, may hold values from 0.5 to 2
- sequence_layernorm_centre: float32 [256], replicated, may hold values from -1 to 1
- asking_projection_matrix: bfloat16 [256, 256], replicated, may hold values from -0.375 to 0.375
- matching_projection_matrix: bfloat16 [256, 256], replicated, may hold values from -0.375 to 0.375
- content_projection_matrix: bfloat16 [256, 256], replicated, may hold values from -0.375 to 0.375
- sigmoid_projection_matrix: bfloat16 [256, 256], replicated, may hold values from -0.375 to 0.375
- gate_offset_bias: float32 [256], replicated, may hold values from -2 to 2
- final_projection_matrix: bfloat16 [256, 256], replicated, may hold values from -0.375 to 0.375
- pairwise_norm_gain: float32 [128], replicated, may hold values from 0.5 to 2
- pairwise_weight: bfloat16 [128, 8], replicated, may hold values from -0.5 to 0.5
Outputs:
- alignment_input_gradient: bfloat16 [128, 1024, 256], P('seq', 'head')
- pairwise_gradient: bfloat16 [1024, 1024, 128], P('seq', 'head')
The draws below stay inside these ranges and needn't reach their ends.
All inputs are finite; a program needn't handle non-finite values.
Results may differ from the reference program's by a relative error of at most 0.012.
The reference program's roundings to bfloat16 on the way count: a program that leaves them out, or rounds other values in their place, can miss the bound.
Values may be sent and summed in bfloat16 or wider, within the bound.
A program may use at most 320 MiB of HBM per device.

```python
import math
import jax
import jax.numpy as jnp
from jax import lax

EMBED_DEPTH = 256
CZ = 128
ATTENTION_TALLY = 8
SUBSPACE_WIDTH = 32
CROP_LENGTH = 1024
SEQUENCE_TALLY = 128


def draw_alignment_rows(key, part):
    base_key = jax.random.fold_in(key, 11)
    random_seed_handle, magnitude_seed_handle = jax.random.split(base_key, 2)
    column_multiplier = jnp.exp(jax.random.uniform(magnitude_seed_handle, (EMBED_DEPTH,), jnp.float32, math.log(0.3), math.log(3.0)))
    tensor_entry = jnp.clip(jax.random.normal(random_seed_handle, (SEQUENCE_TALLY, CROP_LENGTH, EMBED_DEPTH), jnp.float32), -4.0, 4.0)
    return (tensor_entry * column_multiplier).astype(jnp.bfloat16)


def draw_pairwise_features(key, part):
    base_key = jax.random.fold_in(key, 23)
    random_seed_handle, magnitude_seed_handle = jax.random.split(base_key, 2)
    column_multiplier = jnp.exp(jax.random.uniform(magnitude_seed_handle, (CZ,), jnp.float32, math.log(0.3), math.log(3.0)))
    tensor_entry = jnp.clip(jax.random.normal(random_seed_handle, (CROP_LENGTH, CROP_LENGTH, CZ), jnp.float32), -4.0, 4.0)
    return (tensor_entry * column_multiplier).astype(jnp.bfloat16)


def draw_saved_pair_bias(key, part):
    base_key = jax.random.fold_in(key, 37)
    random_seed_handle = jax.random.fold_in(base_key, 0)
    tensor_entry = jnp.clip(0.4 * jax.random.normal(random_seed_handle, (ATTENTION_TALLY, CROP_LENGTH, CROP_LENGTH), jnp.float32), -1.6, 1.6)
    return tensor_entry.astype(jnp.bfloat16)


def strengthened(drawn, stream_key, source, target, parts, factor):
    owner, partner = [(jnp.arange(drawn.shape[axis_at]) // (drawn.shape[axis_at] // parts)).reshape([-1 if axis == axis_at else 1 for axis in range(drawn.ndim)]) for axis_at in (source, target)]
    chosen = jax.random.permutation(stream_key, parts)[partner]
    strong = (owner == chosen) | (owner == (partner + parts // 2) % parts)
    return jnp.where(strong, factor * drawn, drawn)


def levels(own_key, shape, shards, least, largest):
    level = 1.0
    for axis_at, shards_of in shards:
        heights = jax.random.uniform(jax.random.fold_in(jax.random.fold_in(own_key, 6), axis_at), (shards_of,), jnp.float32, least / len(shards), largest / len(shards))
        level = level * jnp.repeat(jnp.exp(heights), shape[axis_at] // shards_of).reshape((-1,) + (1,) * (len(shape) - 1 - axis_at))
    return level


def scatter_about(rng, dims, width, limit, shards=(), kind=jnp.bfloat16):
    drawn = jax.random.normal(rng, dims, jnp.float32) * width
    if len(shards) > 0:
        drawn = levels(rng, dims, shards, -0.22, 0.18) * drawn
    return jnp.clip(drawn, min=-limit, max=limit).astype(kind)


def heavy_noise(rng, dims, width, reach, pieces, heavy, held_as=jnp.bfloat16):
    array = width * jax.random.normal(rng, dims, jnp.float32)
    if pieces:
        array = array * levels(rng, dims, pieces, -0.22, 0.18)
    return jnp.clip(strengthened(array, jax.random.fold_in(rng, 3), *heavy), -reach, reach).astype(held_as)


def setup_inputs(seed: int = 0) -> dict:
    key_of = jax.random.split(jax.random.key(seed), 15)
    alignment_rows = draw_alignment_rows(jax.random.fold_in(key_of[14], 71), 0)
    upstream_derivative_tensor = heavy_noise(key_of[1], (SEQUENCE_TALLY, CROP_LENGTH, EMBED_DEPTH), 2.0, 12.0, ((1, 16),), (0, 1, 16, 2.0))
    saved_pair_bias = draw_saved_pair_bias(jax.random.fold_in(key_of[14], 71), 0)
    pairwise_features = draw_pairwise_features(jax.random.fold_in(key_of[14], 71), 0)
    sequence_layernorm_scaling = jnp.clip(jnp.exp(jax.random.uniform(key_of[4], (EMBED_DEPTH,), jnp.float32, math.log(0.5), math.log(2.0))), 0.5, 2.0)
    sequence_layernorm_centre = jnp.clip(jax.random.uniform(key_of[5], (EMBED_DEPTH,), jnp.float32, -1.0, 1.0), -1.0, 1.0)
    asking_projection_matrix = scatter_about(key_of[6], (EMBED_DEPTH, ATTENTION_TALLY * SUBSPACE_WIDTH), EMBED_DEPTH ** -0.5, 0.375)
    matching_projection_matrix = scatter_about(key_of[7], (EMBED_DEPTH, ATTENTION_TALLY * SUBSPACE_WIDTH), EMBED_DEPTH ** -0.5, 0.375)
    content_projection_matrix = scatter_about(key_of[8], (EMBED_DEPTH, ATTENTION_TALLY * SUBSPACE_WIDTH), EMBED_DEPTH ** -0.5, 0.375)
    sigmoid_projection_matrix = scatter_about(key_of[9], (EMBED_DEPTH, ATTENTION_TALLY * SUBSPACE_WIDTH), EMBED_DEPTH ** -0.5, 0.375)
    gate_offset_bias = jnp.clip(jax.random.uniform(key_of[10], (ATTENTION_TALLY * SUBSPACE_WIDTH,), jnp.float32, -2.0, 2.0), -2.0, 2.0)
    final_projection_matrix = scatter_about(key_of[11], (ATTENTION_TALLY * SUBSPACE_WIDTH, EMBED_DEPTH), (ATTENTION_TALLY * SUBSPACE_WIDTH) ** -0.5, 0.375)
    pairwise_norm_gain = jnp.clip(jnp.exp(jax.random.uniform(key_of[12], (CZ,), jnp.float32, math.log(0.5), math.log(2.0))), 0.5, 2.0)
    pairwise_weight = scatter_about(key_of[13], (CZ, ATTENTION_TALLY), CZ ** -0.5, 0.5)
    return dict(alignment_rows=alignment_rows, upstream_derivative_tensor=upstream_derivative_tensor, saved_pair_bias=saved_pair_bias, pairwise_features=pairwise_features, sequence_layernorm_scaling=sequence_layernorm_scaling, sequence_layernorm_centre=sequence_layernorm_centre, asking_projection_matrix=asking_projection_matrix, matching_projection_matrix=matching_projection_matrix, content_projection_matrix=content_projection_matrix, sigmoid_projection_matrix=sigmoid_projection_matrix, gate_offset_bias=gate_offset_bias, final_projection_matrix=final_projection_matrix, pairwise_norm_gain=pairwise_norm_gain, pairwise_weight=pairwise_weight)


epsilon = 1e-05

def layer_statistics(values):
    average = lax.optimization_barrier(jnp.mean(values, axis=-1, keepdims=True))
    centred = values - average
    inverse_deviation = lax.rsqrt(lax.optimization_barrier(jnp.mean(centred * centred, axis=-1, keepdims=True)) + epsilon)
    return (centred * inverse_deviation, inverse_deviation)

def layer_reverse_step(upstream, standardized_values, inverse_deviation):
    first_mean = lax.optimization_barrier(jnp.mean(upstream, axis=-1, keepdims=True))
    second_mean = lax.optimization_barrier(jnp.mean(upstream * standardized_values, axis=-1, keepdims=True))
    return inverse_deviation * (upstream - first_mean - standardized_values * second_mean)

def rounded(values):
    return lax.optimization_barrier(values.astype(jnp.bfloat16)).astype(jnp.float32)

def reference(alignment_rows, upstream_derivative_tensor, saved_pair_bias, pairwise_features, sequence_layernorm_scaling, sequence_layernorm_centre, asking_projection_matrix, matching_projection_matrix, content_projection_matrix, sigmoid_projection_matrix, gate_offset_bias, final_projection_matrix, pairwise_norm_gain, pairwise_weight):
    score_scale = SUBSPACE_WIDTH ** (-0.5)
    piled_arrays = jnp.stack([coefficient_matrix.reshape(EMBED_DEPTH, ATTENTION_TALLY, SUBSPACE_WIDTH) for coefficient_matrix in (asking_projection_matrix, matching_projection_matrix, content_projection_matrix, sigmoid_projection_matrix)], axis=2)
    piled_arrays = piled_arrays.reshape(EMBED_DEPTH, ATTENTION_TALLY, 4 * SUBSPACE_WIDTH).astype(jnp.float32)
    bias_float = saved_pair_bias.astype(jnp.float32)

    def row_reverse_step(pair_bias_gradient, layer_inputs):
        alignment_row, row_gradient = layer_inputs
        standardized_values, inverse_deviation = layer_statistics(alignment_row.astype(jnp.float32))
        normalized_rows = (standardized_values * sequence_layernorm_scaling + sequence_layernorm_centre).astype(jnp.bfloat16)
        query = rounded(score_scale * jnp.dot(normalized_rows, asking_projection_matrix, preferred_element_type=jnp.float32)).reshape(CROP_LENGTH, ATTENTION_TALLY, SUBSPACE_WIDTH)
        keys = rounded(jnp.dot(normalized_rows, matching_projection_matrix, preferred_element_type=jnp.float32)).reshape(CROP_LENGTH, ATTENTION_TALLY, SUBSPACE_WIDTH)
        vals = rounded(jnp.dot(normalized_rows, content_projection_matrix, preferred_element_type=jnp.float32)).reshape(CROP_LENGTH, ATTENTION_TALLY, SUBSPACE_WIDTH)
        gate = jax.nn.sigmoid(jnp.dot(normalized_rows, sigmoid_projection_matrix, preferred_element_type=jnp.float32) + gate_offset_bias).reshape(CROP_LENGTH, ATTENTION_TALLY, SUBSPACE_WIDTH)
        gated_grad = rounded(jnp.dot(row_gradient, final_projection_matrix.T, preferred_element_type=jnp.float32)).reshape(CROP_LENGTH, ATTENTION_TALLY, SUBSPACE_WIDTH)
        logits = jnp.einsum('ihd,jhd->hij', query, keys) + bias_float
        probs = jax.nn.softmax(logits, axis=-1)
        probs_low = rounded(probs)
        attended = jnp.einsum('hij,jhd->ihd', probs_low, vals)
        attended_grad = rounded(gated_grad * gate)
        gate_grad = rounded(gated_grad * attended * gate * (1.0 - gate))
        prob_grad = jnp.einsum('ihd,jhd->hij', attended_grad, vals)
        inner_sum = lax.optimization_barrier(jnp.sum(probs * prob_grad, axis=-1, keepdims=True))
        score_grad = probs * (prob_grad - inner_sum)
        score_low = rounded(score_grad)
        query_grad = rounded(score_scale * jnp.einsum('hij,jhd->ihd', score_low, keys))
        key_grad = rounded(jnp.einsum('hij,ihd->jhd', score_low, query))
        value_grad = rounded(jnp.einsum('hij,ihd->jhd', probs_low, attended_grad))
        grads = jnp.concatenate([query_grad, key_grad, value_grad, gate_grad], axis=-1)
        normalized_gradient = jnp.einsum('ihf,chf->ic', grads, piled_arrays)
        row_output = layer_reverse_step(normalized_gradient * sequence_layernorm_scaling, standardized_values, inverse_deviation).astype(jnp.bfloat16)
        return (pair_bias_gradient + score_grad, row_output)
    pair_bias_gradient, alignment_input_gradient = lax.scan(row_reverse_step, jnp.zeros((ATTENTION_TALLY, CROP_LENGTH, CROP_LENGTH), jnp.float32), (alignment_rows, upstream_derivative_tensor))
    pair_weight = pairwise_weight.astype(jnp.float32)

    def pair_rows(layer_inputs):
        pair_row, bias_row = layer_inputs
        pair_hat, pair_inv = layer_statistics(pair_row.astype(jnp.float32))
        bias_low = rounded(bias_row)
        pair_normed_grad = jnp.einsum('hj,ch->jc', bias_low, pair_weight, precision=lax.Precision.HIGHEST)
        return layer_reverse_step(pair_normed_grad * pairwise_norm_gain, pair_hat, pair_inv).astype(jnp.bfloat16)
    pairwise_gradient = lax.map(pair_rows, (pairwise_features, jnp.transpose(pair_bias_gradient, (1, 0, 2))))
    return (alignment_input_gradient, pairwise_gradient)
```

```python
import jax
import jax.numpy as jnp
from jax import lax
from jax.experimental import pallas as pl
from jax.experimental.pallas import tpu as pltpu
from jax.sharding import PartitionSpec as P


SUBSPACE_WIDTH = 32
LANES = 128
PACK = LANES // SUBSPACE_WIDTH
VMEM_LIMIT = 60 << 20

epsilon = 1e-05


def dot(left, right, left_dim, right_dim):
    return lax.dot_general(
        left, right, (((left_dim,), (right_dim,)), ((), ())), preferred_element_type=jnp.float32
    )


def layer_statistics(values):
    average = jnp.mean(values, axis=-1, keepdims=True)
    centred = values - average
    inverse_deviation = lax.rsqrt(jnp.mean(centred * centred, axis=-1, keepdims=True) + epsilon)
    return (centred * inverse_deviation, inverse_deviation)


def layer_reverse_step(upstream, standardized_values, inverse_deviation):
    first_mean = jnp.mean(upstream, axis=-1, keepdims=True)
    second_mean = jnp.mean(upstream * standardized_values, axis=-1, keepdims=True)
    return inverse_deviation * (upstream - first_mean - standardized_values * second_mean)


def params():
    return pltpu.CompilerParams(vmem_limit_bytes=VMEM_LIMIT)


def upstream_kernel(heads, up_ref, w_ref, *out_refs):
    rows, residues, channels = up_ref.shape
    group = residues // PACK
    total = None
    for k in range(PACK):
        part = up_ref[:, k * group : (k + 1) * group, :].reshape(rows * group, channels)
        term = dot(part, w_ref[k], 1, 0)
        total = term if total is None else total + term
    for h in range(heads):
        out_refs[h][...] = (
            total[:, h * LANES : (h + 1) * LANES].astype(jnp.bfloat16).reshape(rows, group, LANES)
        )


def project_upstream(upstream, out_rows, heads):
    total_rows, residues, channels = upstream.shape
    weight = out_rows.reshape(heads, SUBSPACE_WIDTH, channels)
    select = jnp.eye(PACK, dtype=weight.dtype)
    padded = jnp.einsum("kp,hdc->kchpd", select, weight).reshape(PACK, channels, heads * LANES)
    block = 32
    group = residues // PACK
    return pl.pallas_call(
        lambda *refs: upstream_kernel(heads, *refs),
        grid=(total_rows // block,),
        in_specs=[
            pl.BlockSpec((block, residues, channels), lambda s: (s, 0, 0)),
            pl.BlockSpec((PACK, channels, heads * LANES), lambda s: (0, 0, 0)),
        ],
        out_specs=[pl.BlockSpec((block, group, LANES), lambda s: (s, 0, 0))] * heads,
        out_shape=[jax.ShapeDtypeStruct((total_rows, group, LANES), jnp.bfloat16)] * heads,
        cost_estimate=pl.CostEstimate(
            flops=2 * upstream.size * heads * LANES, bytes_accessed=8 << 20, transcendentals=0
        ),
        compiler_params=params(),
        name="upstream_projection",
    )(upstream, padded)


def rows_kernel(heads, x_ref, gain_ref, centre_ref, w_ref, wg_ref, shift_ref, out_ref, gate_ref):
    hat, _ = layer_statistics(x_ref[...].astype(jnp.float32))
    normed = (hat * gain_ref[...] + centre_ref[...]).astype(jnp.bfloat16)
    width = heads * SUBSPACE_WIDTH
    raw = dot(w_ref[...], normed, 1, 1)
    out_ref[:width, :] = (raw[:width] * SUBSPACE_WIDTH ** (-0.5)).astype(jnp.bfloat16)
    out_ref[width:, :] = raw[width:].astype(jnp.bfloat16)
    gate_ref[...] = jax.nn.sigmoid(dot(normed, wg_ref[...], 1, 0) + shift_ref[...])


def project_rows(rows, gain, centre, stacked, gate_weight, shift, heads):
    count, residues, channels = rows.shape
    width = heads * SUBSPACE_WIDTH
    full = lambda *shape: pl.BlockSpec(shape, lambda s: (0,) * len(shape))
    return pl.pallas_call(
        lambda *refs: rows_kernel(heads, *refs),
        grid=(count,),
        in_specs=[
            pl.BlockSpec((None, residues, channels), lambda s: (s, 0, 0)),
            full(1, channels),
            full(1, channels),
            full(3 * width, channels),
            full(channels, width),
            full(1, width),
        ],
        out_specs=[
            pl.BlockSpec((None, 3 * width, residues), lambda s: (s, 0, 0)),
            pl.BlockSpec((None, residues, width), lambda s: (s, 0, 0)),
        ],
        out_shape=[
            jax.ShapeDtypeStruct((count, 3 * width, residues), jnp.bfloat16),
            jax.ShapeDtypeStruct((count, residues, width), jnp.float32),
        ],
        cost_estimate=pl.CostEstimate(
            flops=30 * rows.size * 4 * width, bytes_accessed=14 << 20, transcendentals=0
        ),
        compiler_params=params(),
        name="row_projection",
    )(rows, gain[None], centre[None], stacked, gate_weight, shift[None])


def block_order(coords, sizes, relative):
    z, x, c = (lax.rem(coords[k] + relative[k], sizes[k]) for k in range(3))
    return (z * sizes[1] + x) * sizes[2] + c


def attention_kernel(
    tile, sizes, parts, head, at_ref, q_ref, k_ref, v_ref, gate_ref, gd_ref, *refs
):
    zs, xs, cs = sizes
    bias_parts, refs = refs[:cs], refs[cs:]
    grads_out, refs = refs[:parts], refs[parts:]
    sum_out, (bias_ref, acc_ref, grads_ref) = refs[:cs], refs[cs:]
    score_scale = SUBSPACE_WIDTH ** (-0.5)
    residues = acc_ref.shape[0]
    span = residues // (zs * xs * cs)
    group = span // PACK
    coords = [at_ref[k] for k in range(3)]
    places = [
        (c, x, z, pl.multiple_of(block_order(coords, sizes, (z, x, c)) * span, span))
        for c in range(cs)
        for x in range(xs)
        for z in range(zs)
    ]

    @pl.when(pl.program_id(0) == 0)
    def _():
        acc_ref[...] = jnp.zeros_like(acc_ref)
        for c, x, z, start in places:
            bias_ref[pl.ds(start, span), :] = bias_parts[c][x, z]

    keys_t = k_ref[...]
    vals_t = v_ref[...]
    key_grad = jnp.zeros((SUBSPACE_WIDTH, residues), jnp.float32)
    value_grad = jnp.zeros((SUBSPACE_WIDTH, residues), jnp.float32)
    lanes = slice(head * SUBSPACE_WIDTH, (head + 1) * SUBSPACE_WIDTH)
    for start in range(0, residues, tile):
        rows = slice(start, start + tile)
        query_t = q_ref[:, rows]
        query = query_t.astype(jnp.float32).T.astype(jnp.bfloat16)
        logits = dot(query, keys_t, 1, 0) + bias_ref[rows, :].astype(jnp.float32)
        top = jnp.max(logits, axis=-1, keepdims=True)
        weights = jnp.exp(logits - top)
        share = 1.0 / jnp.sum(weights, axis=-1, keepdims=True)
        weights_low = weights.astype(jnp.bfloat16)
        attended = dot(weights_low, vals_t, 1, 1) * share
        gate = gate_ref[rows, lanes]
        packed = gd_ref[start // PACK : (start + tile) // PACK, :].astype(jnp.float32)
        grad = jnp.concatenate(
            [
                packed[b * group : (b + 1) * group, k * SUBSPACE_WIDTH : (k + 1) * SUBSPACE_WIDTH]
                for b in range(tile // span)
                for k in range(PACK)
            ],
            axis=0,
        )
        out_grad = (grad * gate).astype(jnp.bfloat16).astype(jnp.float32)
        scaled = out_grad * share
        inner = jnp.sum(scaled * attended, axis=-1, keepdims=True)
        prob_grad = dot(scaled.astype(jnp.bfloat16), vals_t, 1, 0)
        score_grad = weights * (prob_grad - inner)
        acc_ref[rows, :] += score_grad
        score_low = score_grad.astype(jnp.bfloat16)
        query_grad = score_scale * dot(score_low, keys_t, 1, 1)
        key_grad += dot(query_t, score_low, 1, 0)
        value_grad += dot(scaled.T.astype(jnp.bfloat16), weights_low, 1, 0)
        gate_grad = grad * attended * gate * (1.0 - gate)
        grads_ref[0, :, rows] = query_grad.T.astype(jnp.bfloat16)
        grads_ref[3, :, rows] = gate_grad.T.astype(jnp.bfloat16)
    grads_ref[1] = key_grad.astype(jnp.bfloat16)
    grads_ref[2] = value_grad.astype(jnp.bfloat16)
    length = residues // parts
    for k in range(parts):
        begin = pl.multiple_of(lax.rem(at_ref[3] + k, parts) * length, length)
        for which in range(4):
            grads_out[k][which * SUBSPACE_WIDTH : (which + 1) * SUBSPACE_WIDTH, :] = grads_ref[
                which, :, pl.ds(begin, length)
            ]

    @pl.when(pl.program_id(0) == pl.num_programs(0) - 1)
    def _():
        for c, x, z, start in places:
            sum_out[c][x, z] = acc_ref[pl.ds(start, span), :].astype(jnp.bfloat16)


def attention_reverse(head, at, sizes, parts, projected, gate, gated_grad, bias_parts):
    rows, _, _, width, residues = projected.shape
    zs, xs, cs = sizes
    span = residues // (zs * xs * cs)
    tile = 256

    def part(which):
        return pl.BlockSpec(
            (None, None, None, width, residues), lambda s, at: (s, which, head, 0, 0)
        )

    row = lambda a: pl.BlockSpec((None,) + a.shape[1:], lambda s, at: (s, 0, 0))
    pieces = pl.BlockSpec((xs, zs, span, residues), lambda s, at: (0, 0, 0, 0))
    place, bias_parts = bias_parts
    bias_block = pl.BlockSpec(
        (xs, zs, None, span, residues), lambda s, at: (0, 0, place, 0, 0)
    )
    square = rows * residues * residues
    length = residues // parts
    outs = pl.pallas_call(
        lambda *refs: attention_kernel(tile, sizes, parts, head, *refs),
        grid_spec=pltpu.PrefetchScalarGridSpec(
            num_scalar_prefetch=1,
            grid=(rows,),
            in_specs=[part(0), part(1), part(2), row(gate), row(gated_grad)] + [bias_block] * cs,
            out_specs=[pl.BlockSpec((None, 4 * width, length), lambda s, at: (s, 0, 0))] * parts
            + [pieces] * cs,
            scratch_shapes=[
                pltpu.VMEM((residues, residues), jnp.bfloat16),
                pltpu.VMEM((residues, residues), jnp.float32),
                pltpu.VMEM((4, width, residues), jnp.bfloat16),
            ],
        ),
        out_shape=[jax.ShapeDtypeStruct((rows, 4 * width, length), jnp.bfloat16)] * parts
        + [jax.ShapeDtypeStruct((xs, zs, span, residues), jnp.bfloat16)] * cs,
        cost_estimate=pl.CostEstimate(
            flops=5500 * square, bytes_accessed=12 << 20, transcendentals=square
        ),
        compiler_params=params(),
    )(at, projected, projected, projected, gate, gated_grad, *bias_parts)
    return outs[:parts], outs[parts:]


def final_kernel(count, at_ref, x_ref, gain_ref, w_ref, *refs):
    grad_refs, out_ref = refs[:count], refs[count]
    width = grad_refs[0].shape[0]
    total = None
    for k in range(count):
        term = dot(grad_refs[k][...], w_ref[k * width : (k + 1) * width, :], 0, 0)
        total = term if total is None else total + term
    hat, inverse = layer_statistics(x_ref[...].astype(jnp.float32))
    out_ref[...] = layer_reverse_step(total * gain_ref[...], hat, inverse).astype(jnp.bfloat16)


def final_rows(at, rows, gain, weight, grads):
    count, width, length = grads[0].shape
    channels = rows.shape[-1]
    block = lambda s, at: (s, at[3], 0)
    return pl.pallas_call(
        lambda *refs: final_kernel(len(grads), *refs),
        grid_spec=pltpu.PrefetchScalarGridSpec(
            num_scalar_prefetch=1,
            grid=(count,),
            in_specs=[
                pl.BlockSpec((None, length, channels), block),
                pl.BlockSpec((1, channels), lambda s, at: (0, 0)),
                pl.BlockSpec(weight.shape, lambda s, at: (0, 0)),
            ]
            + [pl.BlockSpec((None, width, length), lambda s, at: (s, 0, 0))] * len(grads),
            out_specs=pl.BlockSpec((None, length, channels), lambda s, at: (s, 0, 0)),
        ),
        out_shape=jax.ShapeDtypeStruct((count, length, channels), jnp.bfloat16),
        cost_estimate=pl.CostEstimate(
            flops=4 * count * width * length * channels * len(grads),
            bytes_accessed=12 << 20,
            transcendentals=0,
        ),
        compiler_params=params(),
        name="final_rows",
    )(at, rows, gain[None], weight, *grads)


def pair_kernel(pair_ref, gain_ref, w_ref, bias_ref, out_ref):
    for i in range(pair_ref.shape[0]):
        upstream = dot(bias_ref[:, i, :], w_ref[...], 0, 0) * gain_ref[...]
        hat, inverse = layer_statistics(pair_ref[i].astype(jnp.float32))
        out_ref[i] = layer_reverse_step(upstream, hat, inverse).astype(jnp.bfloat16)


def pair_reverse(pair, gain, weight, bias):
    count, length, channels = pair.shape
    heads = bias.shape[0]
    block = 8
    return pl.pallas_call(
        pair_kernel,
        grid=(count // block,),
        in_specs=[
            pl.BlockSpec((block, length, channels), lambda s: (s, 0, 0)),
            pl.BlockSpec((1, channels), lambda s: (0, 0)),
            pl.BlockSpec((heads, channels), lambda s: (0, 0)),
            pl.BlockSpec((heads, block, length), lambda s: (0, s, 0)),
        ],
        out_specs=pl.BlockSpec((block, length, channels), lambda s: (s, 0, 0)),
        out_shape=jax.ShapeDtypeStruct(pair.shape, jnp.bfloat16),
        cost_estimate=pl.CostEstimate(
            flops=40 * pair.size, bytes_accessed=18 << 20, transcendentals=0
        ),
        compiler_params=params(),
        name="pair_reverse",
    )(pair, gain[None], weight, bias)


def stage_sizes(seq):
    cs = 2 if seq % 2 == 0 else 1
    rest = seq // cs
    xs = 1
    while rest % (xs * 2) == 0 and (xs * 2) * (xs * 2) <= rest:
        xs *= 2
    return rest // xs, xs, cs


def shift(value, sizes, which, step):
    zs, xs, cs = sizes
    pairs = []
    for z in range(zs):
        for x in range(xs):
            for c in range(cs):
                goal = [z, x, c]
                goal[which] = (goal[which] + step) % sizes[which]
                pairs.append(((z * xs + x) * cs + c, (goal[0] * xs + goal[1]) * cs + goal[2]))
    return lax.ppermute(value, "seq", pairs)


def gather_stage(value, sizes, which):
    return [value] + [
        shift(value, sizes, which, sizes[which] - step)
        for step in range(1, sizes[which])
    ]


def add(terms):
    total = terms[0].astype(jnp.float32)
    for term in terms[1:]:
        total = total + term.astype(jnp.float32)
    return total.astype(jnp.bfloat16)


def reduce_stage(pieces, sizes, which):
    return add(
        [pieces[0]]
        + [shift(pieces[step], sizes, which, step) for step in range(1, sizes[which])]
    )


def groups_of(heads):
    gathers = [[0], [1], list(range(2, heads))] if heads > 2 else [[h] for h in range(heads)]
    reduces = [list(range(heads - 2)), [heads - 2], [heads - 1]] if heads > 2 else gathers
    return gathers, reduces


def per_device(
    sizes,
    parts,
    alignment_rows,
    upstream_derivative_tensor,
    saved_pair_bias,
    pairwise_features,
    sequence_layernorm_scaling,
    sequence_layernorm_centre,
    asking_projection_matrix,
    matching_projection_matrix,
    content_projection_matrix,
    sigmoid_projection_matrix,
    gate_offset_bias,
    final_projection_matrix,
    pairwise_norm_gain,
    pairwise_weight,
):
    heads = saved_pair_bias.shape[0]
    all_heads = pairwise_weight.shape[1]
    count, residues, channels = alignment_rows.shape
    width = heads * SUBSPACE_WIDTH
    zs, xs, cs = sizes
    me = lax.axis_index("seq")
    part = lax.axis_index("head")
    at = jnp.stack([me // (xs * cs), (me // cs) % xs, me % cs, part]).astype(jnp.int32)
    first_col = part * width
    local = lambda matrix: lax.dynamic_slice_in_dim(matrix, first_col, width, 1)
    gathers, reduces = groups_of(heads)

    biases = [None] * heads
    for group in gathers:
        low = saved_pair_bias[group[0] : group[-1] + 1]
        low = jnp.stack(gather_stage(low, sizes, 0))
        wide = jnp.stack(gather_stage(low, sizes, 1))
        both = gather_stage(wide, sizes, 2)
        for place, head in enumerate(group):
            biases[head] = (place, both)
    out_rows = lax.dynamic_slice_in_dim(final_projection_matrix, first_col, width, 0)
    projected_up = project_upstream(upstream_derivative_tensor, out_rows, heads)
    gated = []
    for value in projected_up:
        gated.append(lax.all_to_all(value, "seq", split_axis=0, concat_axis=1, tiled=True))
    stacked = jnp.concatenate(
        [
            local(asking_projection_matrix),
            local(matching_projection_matrix),
            local(content_projection_matrix),
        ],
        axis=1,
    ).T
    projected, gate = project_rows(
        alignment_rows,
        sequence_layernorm_scaling,
        sequence_layernorm_centre,
        stacked,
        local(sigmoid_projection_matrix),
        lax.dynamic_slice_in_dim(gate_offset_bias, first_col, width, 0),
        heads,
    )
    projected = projected.reshape(count, 3, heads, SUBSPACE_WIDTH, residues)

    ring = lambda step: [(k, (k + step) % parts) for k in range(parts)]
    length = residues // parts
    grads = [[None] * heads for _ in range(parts)]
    chips = []
    for head in range(heads):
        split, pieces = attention_reverse(
            head, at, sizes, parts, projected, gate, gated[head], biases[head]
        )
        grads[0][head] = split[0]
        for k in range(1, parts):
            grads[k][head] = lax.ppermute(split[k], "head", ring(k))
        chips.append(reduce_stage(pieces, sizes, 2))
    totals = []
    for group in reduces:
        line = reduce_stage(
            [jnp.stack([chips[h][k] for h in group], axis=1) for k in range(xs)], sizes, 1
        )
        totals.append(reduce_stage([line[k] for k in range(zs)], sizes, 0))
    totals = [jnp.concatenate(totals[:-1]), totals[-1]] if len(totals) > 1 else totals
    sums = [[] for _ in range(parts)]
    for total in totals:
        for k in range(parts):
            block = lax.dynamic_slice_in_dim(total, ((part + k) % parts) * length, length, 2)
            sums[k].append(lax.ppermute(block, "head", ring(k)) if k else block)

    piled = jnp.stack(
        [
            matrix.reshape(channels, all_heads, SUBSPACE_WIDTH)
            for matrix in (
                asking_projection_matrix,
                matching_projection_matrix,
                content_projection_matrix,
                sigmoid_projection_matrix,
            )
        ],
        axis=2,
    )
    order = (part - jnp.arange(parts)) % parts
    weight = piled.reshape(channels, parts, heads * 4 * SUBSPACE_WIDTH).transpose(1, 2, 0)
    weight = weight[order].reshape(all_heads * 4 * SUBSPACE_WIDTH, channels)
    alignment_input_gradient = final_rows(
        at,
        alignment_rows,
        sequence_layernorm_scaling,
        weight,
        [g for group in grads for g in group],
    )
    pair_weight = pairwise_weight.T.reshape(parts, heads, -1)[order].reshape(all_heads, -1)
    pairwise_gradient = pair_reverse(
        pairwise_features,
        pairwise_norm_gain,
        pair_weight,
        jnp.concatenate([s for group in sums for s in group]),
    )
    return (alignment_input_gradient, pairwise_gradient)


def solution(mesh):
    placed = (
        P("seq", None, None),
        P(None, "seq", None),
        P("head", "seq", None),
        P("seq", "head", None),
    ) + (P(),) * 10
    sizes = stage_sizes(mesh.shape["seq"])
    parts = mesh.shape["head"]

    def body(*arrays):
        return per_device(sizes, parts, *arrays)

    return jax.shard_map(
        body,
        mesh=mesh,
        in_specs=placed,
        out_specs=(P("seq", "head", None), P("seq", "head", None)),
        check_vma=False,
    )
```
